32 devices in a mesh: space: 8 (over z, y), freq: 4 (over x, core).
Axes of the slice: x: 2, y: 2, z: 4, core: 2. Of those that a mesh axis runs over, the one named last changes fastest.
Arguments:
- forcing: bfloat16 [4, 32, 8, 8, 1536], P(None, 'freq', None, 'space'), may hold values from -36 to 36
- base_harm: float32 [7, 2, 8, 1536], P(None, None, 'space'), may hold values from -6 to 6
- mixing: float32 [7, 4, 4], replicated, may hold values from -3 to 3
- mean_flow: float32 [1536], replicated, may hold values from 0.2 to 1.2
- harm_lo: int32 [1], replicated, may hold values from -20 to -9
- couple_flags: int32 [32, 7], P('freq'), may hold values 0 or 1
Outputs:
- response: bfloat16 [4, 32, 8, 8, 1536], P(None, 'freq', None, 'space')
- gram_matrix: float32 [4, 4], replicated
The draws below stay inside these ranges and needn't reach their ends.
All inputs are finite; a program needn't handle non-finite values. No bound on the sum of `couple_flags` on one device may be relied on, other than what follows from the above.
Results may differ from the reference program's by a relative error of at most 0.004.
Values may be sent and summed in bfloat16 or wider, within the bound.
No kernel may reach another device: no remote copies, remote signals or barrier semaphores. Data moves between devices by JAX's collectives and lax.ppermute only.
A program may use at most 128 MiB of HBM per device.

```python
import jax
import jax.numpy as jnp
from jax import lax

S = 4
H = 32
V = 4
MODES = 7
NY = 32
NZ = 48
NX = 8
NYZ = 1536


def draw_forcing(key, part):
    first = jax.random.fold_in(key, 0)
    dims_all = (S, H, 2 * V, NX, NY * NZ)
    rise_x = 1.0 + 2.0 * jnp.arange(NX, dtype=jnp.float32) / (NX - 1)
    rise_h = 1.0 + 2.0 * jnp.arange(H, dtype=jnp.float32) / (H - 1)
    scaling = rise_h[None, :, None, None, None] * rise_x[None, None, None, :, None]
    values = jnp.clip(jax.random.normal(first, dims_all, jnp.float32), -4.0, 4.0) * scaling
    return values.astype(jnp.bfloat16)


def plant(entries, own_key, low, largest):
    index_at = [jax.random.randint(jax.random.fold_in(own_key, axis), (), 0, length) for axis, length in enumerate(entries.shape)]
    longest = entries.shape.index(max(entries.shape))
    neighbour = index_at[:longest] + [(index_at[longest] + 1) % entries.shape[longest]] + index_at[longest + 1:]
    return entries.at[tuple(index_at)].set(low).at[tuple(neighbour)].set(largest)


def block_levels(key, shape, pieces, low, high):
    gain = 1.0
    for dim, blocks in pieces:
        draws = jax.random.uniform(jax.random.fold_in(jax.random.fold_in(key, 6), dim), (blocks,), jnp.float32, low / len(pieces), high / len(pieces))
        gain = gain * jnp.repeat(jnp.exp(draws), shape[dim] // blocks).reshape((-1,) + (1,) * (len(shape) - 1 - dim))
    return gain


def centred(stream_key, dims, scale, reach, shards=(), kind=jnp.bfloat16):
    entries = scale * jax.random.normal(stream_key, dims, jnp.float32)
    if shards:
        entries = entries * block_levels(stream_key, dims, shards, -0.22, 0.18)
    return jnp.clip(entries, -reach, reach).astype(kind)


def setup_inputs(seed: int = 0) -> dict:
    key_list = jax.random.split(jax.random.key(seed), 7)
    forcing = draw_forcing(jax.random.fold_in(key_list[6], 71), 0)
    base_harm = centred(key_list[1], (MODES, 2, NX, NYZ), 0.4, 6.0, ((2, 8),), jnp.float32)
    mixing = centred(key_list[2], (MODES, V, V), V ** -0.5, 3.0, (), jnp.float32)
    mean_flow = jnp.clip(jax.random.uniform(key_list[3], (NYZ,), jnp.float32, 0.2, 1.2), 0.2, 1.2)
    harm_lo = jax.random.randint(key_list[4], (1,), -20, -8).astype(jnp.int32)
    couple_flags = plant((jax.random.randint(key_list[5], (H, MODES), 0, 4) < 3).astype(jnp.int32), jax.random.fold_in(key_list[5], 1), 0, 1)
    return dict(forcing=forcing, base_harm=base_harm, mixing=mixing, mean_flow=mean_flow, harm_lo=harm_lo, couple_flags=couple_flags)


OMEGA = 0.05
VISCOSITY = 0.25


def crossflow(values, stream):
    cells = NY * NZ
    position = jnp.arange(cells, dtype=jnp.int32)
    span_pos = position % NZ
    wake_pos = position // NZ
    span_up = jnp.where(span_pos == NZ - 1, jnp.roll(values, NZ - 1, -1), jnp.roll(values, -1, -1))
    span_down = jnp.where(span_pos == 0, jnp.roll(values, 1 - NZ, -1), jnp.roll(values, 1, -1))
    wake_up = jnp.where(wake_pos == NY - 1, 0.0, jnp.roll(values, -NZ, -1))
    wake_down = jnp.where(wake_pos == 0, 0.0, jnp.roll(values, NZ, -1))
    return VISCOSITY * (wake_up + wake_down + span_up + span_down - 6.0 * values)


def streamwise(left_vals, right_vals, stream):
    return (VISCOSITY + 0.5 * stream) * left_vals + (VISCOSITY - 0.5 * stream) * right_vals


def rotation(values, frequency):
    spin_rate = (OMEGA * frequency)[:, None, None, None]
    real_part = values[..., :V, :, :]
    imag_part = values[..., V:, :, :]
    return jnp.concatenate([-spin_rate * imag_part, spin_rate * real_part], axis=-3)


def coupling(padded, base_modes, mixing, couplers):
    count_h = couplers.shape[0]
    summed = None
    for j in range(7):
        offset = j - 3
        source = lax.slice_in_dim(padded, 3 - offset, 3 - offset + count_h, axis=padded.ndim - 4)
        halves = source.reshape(source.shape[:-3] + (2, V) + source.shape[-2:])
        blended = jnp.einsum("vw,...cwxn->...cvxn", mixing[j], halves, precision=lax.Precision.HIGHEST)
        base_re = base_modes[j, 0]
        base_im = base_modes[j, 1]
        mix_re = blended[..., 0, :, :, :]
        mix_im = blended[..., 1, :, :, :]
        product_term = jnp.stack([base_re * mix_re - base_im * mix_im, base_re * mix_im + base_im * mix_re], axis=-4)
        weights = couplers[:, j].astype(jnp.float32)[:, None, None, None, None]
        contrib = weights * product_term
        summed = contrib if summed is None else summed + contrib
    return summed.reshape(summed.shape[:-5] + (count_h, 2 * V) + summed.shape[-2:])


def one_forcing(values, base_modes, mixing, couplers, stream, frequency):
    widened = values.astype(jnp.float32)
    zero_plane = jnp.zeros_like(widened[:, :, :1])
    left_vals = jnp.concatenate([zero_plane, widened[:, :, :-1]], axis=2)
    right_vals = jnp.concatenate([widened[:, :, 1:], zero_plane], axis=2)
    spatial = crossflow(widened, stream) + streamwise(left_vals, right_vals, stream)
    padded = jnp.pad(widened, ((3, 3), (0, 0), (0, 0), (0, 0)))
    result = rotation(widened, frequency) - spatial - coupling(padded, base_modes, mixing, couplers)
    return result.astype(jnp.bfloat16)


def reference(forcing, base_harm, mixing, mean_flow, harm_lo, couple_flags):
    frequency = (harm_lo[0] + jnp.arange(H, dtype=jnp.int32)).astype(jnp.float32)
    response = lax.map(lambda item: one_forcing(item, base_harm, mixing, couple_flags, mean_flow, frequency), forcing)
    flattened = response.reshape(S, -1)
    cells_all = H * 2 * V * NX * NY * NZ
    gram_matrix = jnp.dot(flattened, flattened.T, preferred_element_type=jnp.float32) / cells_all
    return response, gram_matrix
```

```python
import functools

import jax
import jax.numpy as jnp
from jax import lax
from jax.experimental import pallas as pl
from jax.experimental.pallas import tpu as pltpu
from jax.sharding import PartitionSpec as P

V = 4
NY = 32
NZ = 48
MODES = 7
REACH = 3

OMEGA = 0.05
VISCOSITY = 0.25

TILE = 256
HALO_ROWS = 32


def crossflow_tiles():
    tiles = NY * NZ // TILE
    keys = {}
    for j in range(tiles):
        for i in (j - 1, j, j + 1):
            if 0 <= i < tiles:
                keys.setdefault((i - j, (j * TILE) % NZ), len(keys))
    return keys


def prepare_kernel(f_ref, mix_ref, flag_ref, freq_ref, acc_ref, w_ref, lap_ref, *, rows, count_h):
    f32 = jnp.float32
    keys = crossflow_tiles()
    for (offset, phase), at in keys.items():
        source = lax.broadcasted_iota(jnp.int32, (TILE, TILE), 0) + offset * TILE + phase
        target = lax.broadcasted_iota(jnp.int32, (1, TILE), 1) + phase
        pos = target % NZ
        up = jnp.where(pos == NZ - 1, target - (NZ - 1), target + 1)
        down = jnp.where(pos == 0, target + (NZ - 1), target - 1)
        gap = source - target
        near = (source == up) | (source == down) | (gap == NZ) | (gap == -NZ)
        block = jnp.where(gap == 0, 6.0 * VISCOSITY, jnp.where(near, -VISCOSITY, 0.0))
        lap_ref[at] = block.astype(jnp.bfloat16)
    tiles = NY * NZ // TILE
    for j in range(tiles):
        total = None
        for i in (j - 1, j, j + 1):
            if 0 <= i < tiles:
                part = jnp.dot(
                    f_ref[:, i * TILE : (i + 1) * TILE],
                    lap_ref[keys[(i - j, (j * TILE) % NZ)]],
                    preferred_element_type=f32,
                )
                total = part if total is None else total + part
        acc_ref[:, j * TILE : (j + 1) * TILE] = total

    width = rows + 2 * HALO_ROWS
    row = lax.broadcasted_iota(jnp.int32, (8, width), 0)
    col = lax.broadcasted_iota(jnp.int32, (8, width), 1)
    row_v, col_v = row % V, col % V
    same = (row // V) == ((col // V) % 2)
    harm = col // 8

    def put(at, value):
        high = value.astype(jnp.bfloat16)
        low = (value - high.astype(f32)).astype(jnp.bfloat16)
        w_ref[at : at + 8, 0:width] = high
        w_ref[at : at + 8, width : 2 * width] = low

    def slab(k):
        if k < 0:
            return count_h + (k + REACH)
        if k >= count_h:
            return count_h + HALO_ROWS // 8 + (k - count_h)
        return k

    for m in range(MODES):
        mixed = jnp.zeros((8, width), f32)
        for v in range(V):
            for w in range(V):
                mixed = jnp.where((row_v == v) & (col_v == w), -mix_ref[m, v * V + w], mixed)
        mixed = jnp.where(same, mixed, 0.0)
        for k in range(count_h):
            weight = flag_ref[k, m].astype(f32)
            put((m * count_h + k) * 8, jnp.where(harm == slab(k - (m - REACH)), mixed * weight, 0.0))
    sign = jnp.where(row < V, -1.0, 1.0)
    for k in range(count_h):
        rate = OMEGA * (freq_ref[0] + k).astype(f32)
        on = (harm == k) & (row_v == col_v) & jnp.logical_not(same)
        put((MODES * count_h + k) * 8, jnp.where(on, sign * rate, 0.0))


def couple_kernel(f_ref, before_ref, after_ref, w_ref, base_ref, start_ref, out_ref, x_ref, *, rows, count_h):
    f32 = jnp.float32
    width = rows + 2 * HALO_ROWS
    halo = REACH * 8
    lanes = x_ref.shape[1]
    empty = jnp.zeros((HALO_ROWS - halo, lanes), f32)
    around = jnp.concatenate(
        [before_ref[0].astype(f32), empty, after_ref[0].astype(f32), empty], axis=0
    ).astype(jnp.bfloat16)
    own = f_ref[0]
    for at in (0, width):
        x_ref[at : at + rows, :] = own
        x_ref[at + rows : at + width, :] = around
    row = lax.broadcasted_iota(jnp.int32, (8, TILE), 0)
    for j in range(lanes // TILE):
        cut = slice(j * TILE, (j + 1) * TILE)
        mixed = jnp.dot(w_ref[...], x_ref[:, cut], preferred_element_type=f32)
        real = [jnp.broadcast_to(base_ref[2 * m : 2 * m + 1, cut], (8, TILE)) for m in range(MODES)]
        imag = [jnp.broadcast_to(base_ref[2 * m + 1 : 2 * m + 2, cut], (8, TILE)) for m in range(MODES)]
        imag = [jnp.where(row < V, b, -b) for b in imag]
        for k in range(count_h):
            at = (MODES * count_h + k) * 8
            straight = start_ref[0, k * 8 : k * 8 + 8, cut] + mixed[at : at + 8]
            crossed = None
            for m in range(MODES):
                at = (m * count_h + k) * 8
                straight = straight + real[m] * mixed[at : at + 8]
                turn = imag[m] * mixed[at : at + 8]
                crossed = turn if crossed is None else crossed + turn
            out_ref[0, k * 8 : k * 8 + 8, cut] = straight + pltpu.roll(crossed, V, 0)


def finish_kernel(*refs, count_s, scale):
    f32 = jnp.float32
    parts, flows = refs[:count_s], refs[count_s : 2 * count_s]
    out_ref, gram_ref = refs[2 * count_s :]
    rows, lanes = parts[0].shape[1:]
    pairs = [(s, t) for s in range(count_s) for t in range(s, count_s)]

    def step(i, sums):
        at = pl.multiple_of(i * 16, 16)
        cells = []
        for s in range(count_s):
            value = parts[s][0, pl.ds(at, 16), :] - flows[s][0, pl.ds(at, 16), :].astype(f32)
            value = value.astype(jnp.bfloat16)
            out_ref[s, pl.ds(at, 16), :] = value
            cells.append(value.astype(f32))
        new = []
        for (s, t), total in zip(pairs, sums):
            product = cells[s] * cells[t]
            folded = product[0:8] + product[8:16]
            piece = folded[:, 0:128]
            for c in range(1, lanes // 128):
                piece = piece + folded[:, c * 128 : (c + 1) * 128]
            new.append(total + piece)
        return tuple(new)

    sums = lax.fori_loop(0, rows // 16, step, tuple(jnp.zeros((8, 128), f32) for _ in pairs))
    at_s = lax.broadcasted_iota(jnp.int32, (count_s, count_s), 0)
    at_t = lax.broadcasted_iota(jnp.int32, (count_s, count_s), 1)
    gram = jnp.zeros((count_s, count_s), f32)
    for (s, t), total in zip(pairs, sums):
        value = jnp.sum(total, keepdims=True) * scale
        here = ((at_s == s) & (at_t == t)) | ((at_s == t) & (at_t == s))
        gram = jnp.where(here, value, gram)
    gram_ref[...] = gram


def summed_over(value, axes):
    for axis in axes:
        count = lax.axis_size(axis)
        if count & (count - 1):
            value = lax.psum(value, axis)
            continue
        step = 1
        while step < count:
            value = value + lax.ppermute(value, axis, [(i, i ^ step) for i in range(count)])
            step *= 2
    return value


def local(forcing, base_harm, mixing, mean_flow, harm_lo, couple_flags):
    count_s, count_h, _, planes, cells = forcing.shape
    slabs = lax.axis_size("space")
    blocks = lax.axis_size("freq")
    assert planes == 1 and slabs % 2 == 0
    rows = count_h * 2 * V
    f32 = jnp.float32
    values = forcing.reshape(count_s, rows, cells)

    skip = [(i, i + 2) for i in range(1, slabs - 2, 2)] + [(i, i - 2) for i in range(2, slabs, 2)]
    swap = [(i, i ^ 1) for i in range(slabs)]
    odd = lax.axis_index("space") % 2 == 1
    from_left = (VISCOSITY + 0.5 * mean_flow)[None, None]
    from_right = (VISCOSITY - 0.5 * mean_flow)[None, None]
    own_gain = jnp.where(odd, from_right, from_left)
    far_gain = jnp.where(odd, from_left, from_right)
    flows = []
    for s in range(count_s):
        own = values[s : s + 1]
        far = lax.ppermute(own, "space", skip)
        both = own_gain * own.astype(f32) + far_gain * far.astype(f32)
        flows.append(lax.ppermute(both.astype(jnp.bfloat16), "space", swap))

    halo = REACH * 2 * V
    before = lax.ppermute(values[:, rows - halo :], "freq", [(i, i + 1) for i in range(blocks - 1)])
    after = lax.ppermute(values[:, :halo], "freq", [(i + 1, i) for i in range(blocks - 1)])

    first = harm_lo + lax.axis_index("freq") * count_h
    mixed_rows = (MODES + 1) * rows
    width = 2 * (rows + 2 * HALO_ROWS)
    vmem = pl.BlockSpec(memory_space=pltpu.VMEM)
    smem = pl.BlockSpec(memory_space=pltpu.SMEM)
    start, weights = pl.pallas_call(
        functools.partial(prepare_kernel, rows=rows, count_h=count_h),
        out_shape=(
            jax.ShapeDtypeStruct((count_s * rows, cells), f32),
            jax.ShapeDtypeStruct((mixed_rows, width), jnp.bfloat16),
        ),
        in_specs=[vmem, smem, smem, smem],
        out_specs=(vmem, vmem),
        scratch_shapes=[pltpu.VMEM((len(crossflow_tiles()), TILE, TILE), jnp.bfloat16)],
        name="prepare",
    )(values.reshape(count_s * rows, cells), mixing.reshape(MODES, V * V), couple_flags, first)
    start = start.reshape(count_s, rows, cells)
    base = base_harm.reshape(2 * MODES, cells)

    parts = []
    for s in range(count_s):
        one = lambda *_, s=s: (s, 0, 0)
        parts.append(
            pl.pallas_call(
                functools.partial(couple_kernel, rows=rows, count_h=count_h),
                out_shape=jax.ShapeDtypeStruct((1, rows, cells), f32),
                grid=(1,),
                in_specs=[
                    pl.BlockSpec((1, rows, cells), one),
                    pl.BlockSpec((1, halo, cells), one),
                    pl.BlockSpec((1, halo, cells), one),
                    pl.BlockSpec((mixed_rows, width), lambda *_: (0, 0)),
                    pl.BlockSpec((2 * MODES, cells), lambda *_: (0, 0)),
                    pl.BlockSpec((1, rows, cells), one),
                ],
                out_specs=pl.BlockSpec((1, rows, cells), lambda *_: (0, 0, 0)),
                scratch_shapes=[pltpu.VMEM((width, cells), jnp.bfloat16)],
                name="couple",
            )(values, before, after, weights, base, start)
        )

    cells_all = count_h * blocks * 2 * V * planes * slabs * cells
    response, gram = pl.pallas_call(
        functools.partial(finish_kernel, count_s=count_s, scale=1.0 / cells_all),
        out_shape=(
            jax.ShapeDtypeStruct((count_s, rows, cells), jnp.bfloat16),
            jax.ShapeDtypeStruct((count_s, count_s), f32),
        ),
        in_specs=[vmem] * (2 * count_s),
        out_specs=(vmem, vmem),
        name="finish",
    )(*parts, *flows)
    return response.reshape(forcing.shape), summed_over(gram, ("freq", "space"))


def solution(mesh):
    return jax.shard_map(
        local,
        mesh=mesh,
        in_specs=(
            P(None, "freq", None, "space", None),
            P(None, None, "space", None),
            P(),
            P(),
            P(),
            P("freq", None),
        ),
        out_specs=(P(None, "freq", None, "space", None), P()),
        check_vma=False,
    )
```

```python
import functools
import math

import jax
import jax.numpy as jnp
from jax import lax
from jax.experimental import pallas as pl
from jax.experimental.pallas import tpu as pltpu
from jax.sharding import PartitionSpec as P


V = 4
NZ = 48
MODES = 7
REACH = 3

OMEGA = 0.05
VISCOSITY = 0.25

TILE = 256
LANES = 128
GRANT = 8 * 2**20
HALO_ROWS = 32


def split_kernel(f_ref, *refs):
    *planes, sems = refs
    copies = [pltpu.make_async_copy(f_ref.at[s], plane, sems.at[s]) for s, plane in enumerate(planes)]
    for copy in copies:
        copy.start()
    for copy in copies:
        copy.wait()


def edges_kernel(f_ref, last_ref, first_ref, sems):
    rows, halo = f_ref.shape[1], last_ref.shape[1]
    copies = [
        pltpu.make_async_copy(f_ref.at[:, rows - halo : rows], last_ref, sems.at[0]),
        pltpu.make_async_copy(f_ref.at[:, 0:halo], first_ref, sems.at[1]),
    ]
    for copy in copies:
        copy.start()
    for copy in copies:
        copy.wait()


def gains(mean_ref, slab_ref, slabs):
    slab = slab_ref[0]
    odd = slab % 2 == 1
    inside = jnp.where(odd, slab < slabs - 1, slab > 0).astype(jnp.float32)
    tilt = jnp.where(odd, 0.5, -0.5).astype(jnp.float32) * mean_ref[...]
    return VISCOSITY + tilt, (VISCOSITY - tilt) * inside


def join_kernel(own_ref, far_ref, mean_ref, slab_ref, out_ref, *, slabs):
    slab = slab_ref[0]
    odd = slab % 2 == 1
    inside = jnp.where(odd, slab > 1, slab < slabs - 2).astype(jnp.float32)
    tilt = jnp.where(odd, -0.5, 0.5).astype(jnp.float32) * mean_ref[...]
    far_gain = (VISCOSITY - tilt) * inside
    total = (VISCOSITY + tilt) * own_ref[...].astype(jnp.float32)
    total = total + far_gain * far_ref[...].astype(jnp.float32)
    out_ref[...] = total.astype(jnp.bfloat16)


def prepare_kernel(*refs, count_s, count_h, blocks):
    f32 = jnp.float32
    f_refs = refs[:count_s]
    mix_ref, flag_ref, low_ref, block_ref = refs[count_s : count_s + 4]
    *acc_refs, w_ref, lap_ref = refs[count_s + 4 :]
    rows, cells = f_refs[0].shape
    phases = lap_ref.shape[0]
    for p in range(phases):
        start = (p * LANES) % NZ
        source = lax.broadcasted_iota(jnp.int32, (3 * LANES, LANES), 0) + (start - LANES)
        target = lax.broadcasted_iota(jnp.int32, (1, LANES), 1) + start
        pos = target % NZ
        up = jnp.where(pos == NZ - 1, target - (NZ - 1), target + 1)
        down = jnp.where(pos == 0, target + (NZ - 1), target - 1)
        gap = jnp.abs(source - target)
        near = (source == up) | (source == down) | (gap == NZ)
        block = jnp.where(gap == 0, 6.0 * VISCOSITY, jnp.where(near, -VISCOSITY, 0.0))
        lap_ref[p] = block.astype(jnp.bfloat16)
    steps = cells // LANES
    for j in range(steps):
        low, high = max(j - 1, 0), min(j + 2, steps)
        weights = lap_ref[j % phases, (low - j + 1) * LANES : (high - j + 1) * LANES, :]
        for f_ref, acc_ref in zip(f_refs, acc_refs):
            acc_ref[:, j * LANES : (j + 1) * LANES] = jnp.dot(
                f_ref[:, low * LANES : high * LANES], weights, preferred_element_type=f32
            )

    width = rows + 2 * HALO_ROWS
    row = lax.broadcasted_iota(jnp.int32, (8, width), 0)
    col = lax.broadcasted_iota(jnp.int32, (8, width), 1)
    row_v, col_v = row % V, col % V
    same = (row // V) == ((col // V) % 2)
    harm = col // 8

    def put(at, value):
        high = value.astype(jnp.bfloat16)
        low = (value - high.astype(f32)).astype(jnp.bfloat16)
        w_ref[at : at + 16, 0:width] = high
        w_ref[at : at + 16, width : 2 * width] = low

    def slab(k):
        if k < 0:
            return count_h + (k + REACH)
        if k >= count_h:
            return count_h + HALO_ROWS // 8 + (k - count_h)
        return k

    def two(tile):
        return jnp.concatenate([tile(0), tile(1)], axis=0)

    reached = jnp.where(
        harm < count_h,
        1.0,
        jnp.where(
            harm < count_h + HALO_ROWS // 8,
            (block_ref[0] > 0).astype(f32),
            (block_ref[0] < blocks - 1).astype(f32),
        ),
    )
    for m in range(MODES):
        mixed = jnp.zeros((8, width), f32)
        for v in range(V):
            for w in range(V):
                mixed = jnp.where((row_v == v) & (col_v == w), -mix_ref[v, w, m], mixed)
        mixed = jnp.where(same, mixed, 0.0) * reached
        for k in range(0, count_h, 2):
            put(
                (m * count_h + k) * 8,
                two(
                    lambda i: jnp.where(
                        harm == slab(k + i - (m - REACH)),
                        mixed * flag_ref[k + i, m].astype(f32),
                        0.0,
                    )
                ),
            )
    sign = jnp.where(row < V, -1.0, 1.0)
    first = low_ref[0] + block_ref[0] * count_h
    crossed = (row_v == col_v) & jnp.logical_not(same)
    for k in range(0, count_h, 2):
        put(
            (MODES * count_h + k) * 8,
            two(
                lambda i: jnp.where(
                    crossed & (harm == k + i), sign * (OMEGA * (first + k + i).astype(f32)), 0.0
                )
            ),
        )


def couple_kernel(f_ref, before_ref, after_ref, w_ref, base_ref, start_ref, out_ref, x_ref, *, at_s, count_h):
    f32 = jnp.float32
    rows, cells = f_ref.shape
    width = rows + 2 * HALO_ROWS
    empty = jnp.zeros((HALO_ROWS - REACH * 8, cells), f32)
    around = jnp.concatenate(
        [before_ref[at_s].astype(f32), empty, after_ref[at_s].astype(f32), empty], axis=0
    ).astype(jnp.bfloat16)
    own = f_ref[...]
    for at in (0, width):
        x_ref[at : at + rows, :] = own
        x_ref[at + rows : at + width, :] = around
    row = lax.broadcasted_iota(jnp.int32, (8, TILE), 0)
    for j in range(cells // TILE):
        cut = slice(j * TILE, (j + 1) * TILE)
        mixed = jnp.dot(w_ref[...], x_ref[:, cut], preferred_element_type=f32)
        real = [jnp.broadcast_to(base_ref[m, 0, :, cut], (8, TILE)) for m in range(MODES)]
        imag = [jnp.broadcast_to(base_ref[m, 1, :, cut], (8, TILE)) for m in range(MODES)]
        imag = [jnp.where(row < V, b, -b) for b in imag]
        for k in range(count_h):
            at = (MODES * count_h + k) * 8
            straight = start_ref[k * 8 : k * 8 + 8, cut] + mixed[at : at + 8]
            crossed = None
            for m in range(MODES):
                at = (m * count_h + k) * 8
                straight = straight + real[m] * mixed[at : at + 8]
                turn = imag[m] * mixed[at : at + 8]
                crossed = turn if crossed is None else crossed + turn
            out_ref[k * 8 : k * 8 + 8, cut] = straight + pltpu.roll(crossed, V, 0)


def finish_kernel(*refs, count_s, slabs, scale):
    f32 = jnp.float32
    mean_ref, slab_ref, *refs = refs
    parts, flows = refs[:count_s], refs[count_s:-2]
    out_ref, gram_ref = refs[-2:]
    rows, cells = parts[0].shape
    pairs = [(s, t) for s in range(count_s) for t in range(s, count_s)]
    sums = [None] * len(pairs)
    near_gain, far_gain = gains(mean_ref, slab_ref, slabs)
    for c in range(0, cells, LANES):
        cut = slice(c, c + LANES)
        near_here = jnp.broadcast_to(near_gain[:, cut], (16, LANES))
        far_here = jnp.broadcast_to(far_gain[:, cut], (16, LANES))
        for r in range(0, rows, 16):
            values = []
            for s in range(count_s):
                value = parts[s][r : r + 16, cut]
                if s < count_s // 2:
                    value = value - near_here * flows[2 * s][r : r + 16, cut].astype(f32)
                    value = value - far_here * flows[2 * s + 1][r : r + 16, cut].astype(f32)
                else:
                    value = value - flows[s + count_s // 2][r : r + 16, cut].astype(f32)
                value = value.astype(jnp.bfloat16)
                out_ref[s, r : r + 16, cut] = value
                values.append(value.astype(f32))
            for p, (s, t) in enumerate(pairs):
                product = values[s] * values[t]
                sums[p] = product if sums[p] is None else sums[p] + product
    at_s = lax.broadcasted_iota(jnp.int32, (count_s, count_s), 0)
    at_t = lax.broadcasted_iota(jnp.int32, (count_s, count_s), 1)
    gram = jnp.zeros((count_s, count_s), f32)
    for (s, t), total in zip(pairs, sums):
        value = jnp.sum(total, keepdims=True) * scale
        here = ((at_s == s) & (at_t == t)) | ((at_s == t) & (at_t == s))
        gram = jnp.where(here, value, gram)
    gram_ref[...] = gram


def near(*values):
    return [pltpu.with_memory_space_constraint(value, pltpu.VMEM) for value in values]


def far_away(value):
    return pltpu.with_memory_space_constraint(value, pltpu.HBM)


def summed_over(value, axes):
    for axis in axes:
        count = lax.axis_size(axis)
        if count & (count - 1):
            value = lax.psum(value, axis)
            continue
        step = 1
        while step < count:
            value = value + lax.ppermute(value, axis, [(i, i ^ step) for i in range(count)])
            step *= 2
    return value


def local(forcing, base_harm, mixing, mean_flow, harm_lo, couple_flags):
    count_s, count_h, _, planes, cells = forcing.shape
    slabs = lax.axis_size("space")
    blocks = lax.axis_size("freq")
    assert planes == 1 and slabs % 2 == 0 and count_h % 2 == 0
    rows = count_h * 2 * V
    halo = REACH * 2 * V
    f32, bf16 = jnp.float32, jnp.bfloat16
    vmem = pl.BlockSpec(memory_space=pltpu.VMEM)
    smem = pl.BlockSpec(memory_space=pltpu.SMEM)
    whole = pl.BlockSpec(memory_space=pl.ANY)
    slab = lax.axis_index("space").reshape(1)
    block = lax.axis_index("freq").reshape(1)

    apart = [(i, (i + 2 if i % 2 else i - 2) % slabs) for i in range(slabs)]
    swap = [(i, i ^ 1) for i in range(slabs)]

    values = forcing.reshape(count_s, rows, cells)
    forcings = pl.pallas_call(
        split_kernel,
        out_shape=[pltpu.VMEM((rows, cells), bf16)] * count_s,
        in_specs=[whole],
        out_specs=[vmem] * count_s,
        scratch_shapes=[pltpu.SemaphoreType.DMA((count_s,))],
        compiler_params=pltpu.CompilerParams(vmem_limit_bytes=GRANT),
        name="split",
    )(far_away(values))
    last, first = pl.pallas_call(
        edges_kernel,
        out_shape=[pltpu.VMEM((count_s, halo, cells), bf16)] * 2,
        in_specs=[whole],
        out_specs=[vmem] * 2,
        scratch_shapes=[pltpu.SemaphoreType.DMA((2,))],
        compiler_params=pltpu.CompilerParams(vmem_limit_bytes=GRANT),
        name="edges",
    )(far_away(values))

    mean = mean_flow.reshape(1, cells)
    flows = []
    for s in range(count_s // 2):
        beside = lax.ppermute(forcings[s], "space", swap)
        beyond = lax.ppermute(beside, "space", [(j, i) for i, j in apart])
        flows += [beside, beyond]
    for s in range(count_s // 2, count_s):
        beyond = lax.ppermute(forcings[s], "space", apart)
        both = pl.pallas_call(
            functools.partial(join_kernel, slabs=slabs),
            out_shape=pltpu.VMEM((rows, cells), bf16),
            in_specs=[vmem, vmem, vmem, smem],
            out_specs=vmem,
            compiler_params=pltpu.CompilerParams(vmem_limit_bytes=GRANT),
            name="join",
        )(*near(forcings[s], beyond, mean), slab)
        flows.append(lax.ppermute(both, "space", swap))

    one = lax.ppermute(last, "freq", [(i, (i + 1) % blocks) for i in range(blocks)])
    other = lax.ppermute(first, "freq", [((i + 1) % blocks, i) for i in range(blocks)])
    before, after = one, other

    mixed_rows = (MODES + 1) * rows
    width = 2 * (rows + 2 * HALO_ROWS)
    *starts, weights = pl.pallas_call(
        functools.partial(prepare_kernel, count_s=count_s, count_h=count_h, blocks=blocks),
        out_shape=[pltpu.VMEM((rows, cells), f32)] * count_s + [pltpu.VMEM((mixed_rows, width), bf16)],
        in_specs=[vmem] * count_s + [smem] * 4,
        out_specs=[vmem] * (count_s + 1),
        scratch_shapes=[pltpu.VMEM((NZ // math.gcd(LANES, NZ), 3 * LANES, LANES), bf16)],
        compiler_params=pltpu.CompilerParams(vmem_limit_bytes=GRANT),
        name="prepare",
    )(*near(*forcings), mixing.transpose(1, 2, 0), couple_flags, harm_lo, block)

    parts = []
    for s in range(count_s):
        part = pl.pallas_call(
            functools.partial(couple_kernel, at_s=s, count_h=count_h),
            out_shape=pltpu.VMEM((rows, cells), f32),
            in_specs=[vmem] * 6,
            out_specs=vmem,
            scratch_shapes=[pltpu.VMEM((width, cells), bf16)],
            compiler_params=pltpu.CompilerParams(vmem_limit_bytes=GRANT),
            name="couple",
        )(*near(forcings[s], before, after, weights, base_harm, starts[s]))
        parts.append(part)

    cells_all = count_h * blocks * 2 * V * planes * slabs * cells
    response, gram = pl.pallas_call(
        functools.partial(finish_kernel, count_s=count_s, slabs=slabs, scale=1.0 / cells_all),
        out_shape=[pltpu.VMEM((count_s, rows, cells), bf16), pltpu.VMEM((count_s, count_s), f32)],
        in_specs=[vmem, smem] + [vmem] * (count_s + len(flows)),
        out_specs=[vmem] * 2,
        compiler_params=pltpu.CompilerParams(vmem_limit_bytes=GRANT),
        name="finish",
    )(*near(mean), slab, *near(*parts, *flows))
    return response.reshape(forcing.shape), summed_over(gram, ("freq", "space"))


def solution(mesh):
    return jax.shard_map(
        local,
        mesh=mesh,
        in_specs=(
            P(None, "freq", None, "space", None),
            P(None, None, "space", None),
            P(),
            P(),
            P(),
            P("freq", None),
        ),
        out_specs=(P(None, "freq", None, "space", None), P()),
        check_vma=False,
    )
```

```python
import functools
import math

import jax
import jax.numpy as jnp
from jax import lax
from jax.experimental import pallas as pl
from jax.experimental.pallas import tpu as pltpu
from jax.sharding import PartitionSpec as P


V = 4
NZ = 48
MODES = 7
REACH = 3

OMEGA = 0.05
VISCOSITY = 0.25

TILE = 256
LANES = 128
GRANT = 8 * 2**20
HALO_ROWS = 32


def split_kernel(f_ref, *refs, picks):
    *outs, sems = refs
    copies = [pltpu.make_async_copy(f_ref.at[s], out, sems.at[i]) for i, (s, out) in enumerate(zip(picks, outs))]
    for copy in copies:
        copy.start()
    for copy in copies:
        copy.wait()


def edges_kernel(f_ref, *refs, picks):
    *outs, last_ref, first_ref, sems = refs
    rows, halo = f_ref.shape[1], last_ref.shape[1]
    copies = [
        pltpu.make_async_copy(f_ref.at[:, rows - halo : rows], last_ref, sems.at[0]),
        pltpu.make_async_copy(f_ref.at[:, 0:halo], first_ref, sems.at[1]),
    ]
    for i, (s, out) in enumerate(zip(picks, outs)):
        copies.append(pltpu.make_async_copy(f_ref.at[s], out, sems.at[2 + i]))
    for copy in copies:
        copy.start()
    for copy in copies:
        copy.wait()


def gains(mean_ref, slab_ref, slabs):
    slab = slab_ref[0]
    odd = slab % 2 == 1
    inside = jnp.where(odd, slab < slabs - 1, slab > 0).astype(jnp.float32)
    tilt = jnp.where(odd, 0.5, -0.5).astype(jnp.float32) * mean_ref[...]
    return VISCOSITY + tilt, (VISCOSITY - tilt) * inside


def join_kernel(own_ref, far_ref, mean_ref, slab_ref, out_ref, *, slabs):
    slab = slab_ref[0]
    odd = slab % 2 == 1
    inside = jnp.where(odd, slab > 1, slab < slabs - 2).astype(jnp.float32)
    tilt = jnp.where(odd, -0.5, 0.5).astype(jnp.float32) * mean_ref[...]
    far_gain = (VISCOSITY - tilt) * inside
    total = (VISCOSITY + tilt) * own_ref[...].astype(jnp.float32)
    total = total + far_gain * far_ref[...].astype(jnp.float32)
    out_ref[...] = total.astype(jnp.bfloat16)


def prepare_kernel(*refs, count_s, count_h, blocks):
    f32 = jnp.float32
    f_refs = refs[:count_s]
    mix_ref, flag_ref, low_ref, block_ref = refs[count_s : count_s + 4]
    *acc_refs, w_ref, lap_ref = refs[count_s + 4 :]
    rows, cells = f_refs[0].shape
    phases = lap_ref.shape[0]
    for p in range(phases):
        start = (p * LANES) % NZ
        source = lax.broadcasted_iota(jnp.int32, (3 * LANES, LANES), 0) + (start - LANES)
        target = lax.broadcasted_iota(jnp.int32, (1, LANES), 1) + start
        pos = target % NZ
        up = jnp.where(pos == NZ - 1, target - (NZ - 1), target + 1)
        down = jnp.where(pos == 0, target + (NZ - 1), target - 1)
        gap = jnp.abs(source - target)
        near = (source == up) | (source == down) | (gap == NZ)
        block = jnp.where(gap == 0, 6.0 * VISCOSITY, jnp.where(near, -VISCOSITY, 0.0))
        lap_ref[p] = block.astype(jnp.bfloat16)
    steps = cells // LANES
    for j in range(steps):
        low, high = max(j - 1, 0), min(j + 2, steps)
        weights = lap_ref[j % phases, (low - j + 1) * LANES : (high - j + 1) * LANES, :]
        for f_ref, acc_ref in zip(f_refs, acc_refs):
            acc_ref[:, j * LANES : (j + 1) * LANES] = jnp.dot(
                f_ref[:, low * LANES : high * LANES], weights, preferred_element_type=f32
            )

    width = rows + 2 * HALO_ROWS
    row = lax.broadcasted_iota(jnp.int32, (8, width), 0)
    col = lax.broadcasted_iota(jnp.int32, (8, width), 1)
    row_v, col_v = row % V, col % V
    same = (row // V) == ((col // V) % 2)
    harm = col // 8

    def put(at, value):
        high = value.astype(jnp.bfloat16)
        low = (value - high.astype(f32)).astype(jnp.bfloat16)
        w_ref[at : at + 16, 0:width] = high
        w_ref[at : at + 16, width : 2 * width] = low

    def slab(k):
        if k < 0:
            return count_h + (k + REACH)
        if k >= count_h:
            return count_h + HALO_ROWS // 8 + (k - count_h)
        return k

    def two(tile):
        return jnp.concatenate([tile(0), tile(1)], axis=0)

    reached = jnp.where(
        harm < count_h,
        1.0,
        jnp.where(
            harm < count_h + HALO_ROWS // 8,
            (block_ref[0] > 0).astype(f32),
            (block_ref[0] < blocks - 1).astype(f32),
        ),
    )
    for m in range(MODES):
        mixed = jnp.zeros((8, width), f32)
        for v in range(V):
            for w in range(V):
                mixed = jnp.where((row_v == v) & (col_v == w), -mix_ref[v, w, m], mixed)
        mixed = jnp.where(same, mixed, 0.0) * reached
        for k in range(0, count_h, 2):
            put(
                (m * count_h + k) * 8,
                two(
                    lambda i: jnp.where(
                        harm == slab(k + i - (m - REACH)),
                        mixed * flag_ref[k + i, m].astype(f32),
                        0.0,
                    )
                ),
            )
    sign = jnp.where(row < V, -1.0, 1.0)
    first = low_ref[0] + block_ref[0] * count_h
    crossed = (row_v == col_v) & jnp.logical_not(same)
    for k in range(0, count_h, 2):
        put(
            (MODES * count_h + k) * 8,
            two(
                lambda i: jnp.where(
                    crossed & (harm == k + i), sign * (OMEGA * (first + k + i).astype(f32)), 0.0
                )
            ),
        )


def couple_kernel(f_ref, before_ref, after_ref, w_ref, base_ref, start_ref, out_ref, x_ref, *, at_s, count_h):
    f32 = jnp.float32
    rows, cells = f_ref.shape
    width = rows + 2 * HALO_ROWS
    empty = jnp.zeros((HALO_ROWS - REACH * 8, cells), f32)
    around = jnp.concatenate(
        [before_ref[at_s].astype(f32), empty, after_ref[at_s].astype(f32), empty], axis=0
    ).astype(jnp.bfloat16)
    own = f_ref[...]
    for at in (0, width):
        x_ref[at : at + rows, :] = own
        x_ref[at + rows : at + width, :] = around
    row = lax.broadcasted_iota(jnp.int32, (8, TILE), 0)
    for j in range(cells // TILE):
        cut = slice(j * TILE, (j + 1) * TILE)
        mixed = jnp.dot(w_ref[...], x_ref[:, cut], preferred_element_type=f32)
        real = [jnp.broadcast_to(base_ref[m, 0, :, cut], (8, TILE)) for m in range(MODES)]
        imag = [jnp.broadcast_to(base_ref[m, 1, :, cut], (8, TILE)) for m in range(MODES)]
        imag = [jnp.where(row < V, b, -b) for b in imag]
        for k in range(count_h):
            at = (MODES * count_h + k) * 8
            straight = start_ref[k * 8 : k * 8 + 8, cut] + mixed[at : at + 8]
            crossed = None
            for m in range(MODES):
                at = (m * count_h + k) * 8
                straight = straight + real[m] * mixed[at : at + 8]
                turn = imag[m] * mixed[at : at + 8]
                crossed = turn if crossed is None else crossed + turn
            out_ref[k * 8 : k * 8 + 8, cut] = straight + pltpu.roll(crossed, V, 0)


def finish_kernel(*refs, count_s, slabs, scale):
    f32 = jnp.float32
    mean_ref, slab_ref, *refs = refs
    parts, flows = refs[:count_s], refs[count_s:-2]
    out_ref, gram_ref = refs[-2:]
    rows, cells = parts[0].shape
    pairs = [(s, t) for s in range(count_s) for t in range(s, count_s)]
    sums = [None] * len(pairs)
    near_gain, far_gain = gains(mean_ref, slab_ref, slabs)
    for c in range(0, cells, LANES):
        cut = slice(c, c + LANES)
        near_here = jnp.broadcast_to(near_gain[:, cut], (16, LANES))
        far_here = jnp.broadcast_to(far_gain[:, cut], (16, LANES))
        for r in range(0, rows, 16):
            values = []
            for s in range(count_s):
                value = parts[s][r : r + 16, cut]
                if s < count_s // 2:
                    value = value - near_here * flows[2 * s][r : r + 16, cut].astype(f32)
                    value = value - far_here * flows[2 * s + 1][r : r + 16, cut].astype(f32)
                else:
                    value = value - flows[s + count_s // 2][r : r + 16, cut].astype(f32)
                value = value.astype(jnp.bfloat16)
                out_ref[s, r : r + 16, cut] = value
                values.append(value.astype(f32))
            for p, (s, t) in enumerate(pairs):
                product = values[s] * values[t]
                sums[p] = product if sums[p] is None else sums[p] + product
    at_s = lax.broadcasted_iota(jnp.int32, (count_s, count_s), 0)
    at_t = lax.broadcasted_iota(jnp.int32, (count_s, count_s), 1)
    gram = jnp.zeros((count_s, count_s), f32)
    for (s, t), total in zip(pairs, sums):
        value = jnp.sum(total, keepdims=True) * scale
        here = ((at_s == s) & (at_t == t)) | ((at_s == t) & (at_t == s))
        gram = jnp.where(here, value, gram)
    gram_ref[...] = gram


def near(*values):
    return [pltpu.with_memory_space_constraint(value, pltpu.VMEM) for value in values]


def far_away(value):
    return pltpu.with_memory_space_constraint(value, pltpu.HBM)


def local(forcing, base_harm, mixing, mean_flow, harm_lo, couple_flags):
    count_s, count_h, _, planes, cells = forcing.shape
    slabs = lax.axis_size("space")
    blocks = lax.axis_size("freq")
    assert planes == 1 and slabs % 2 == 0 and count_h % 2 == 0
    rows = count_h * 2 * V
    halo = REACH * 2 * V
    f32, bf16 = jnp.float32, jnp.bfloat16
    vmem = pl.BlockSpec(memory_space=pltpu.VMEM)
    smem = pl.BlockSpec(memory_space=pltpu.SMEM)
    whole = pl.BlockSpec(memory_space=pl.ANY)
    slab = lax.axis_index("space").reshape(1)
    block = lax.axis_index("freq").reshape(1)

    apart = [(i, (i + 2 if i % 2 else i - 2) % slabs) for i in range(slabs)]
    swap = [(i, i ^ 1) for i in range(slabs)]

    early = [0, count_s // 2]
    late = [s for s in range(count_s) if s not in early]
    plane = pltpu.VMEM((rows, cells), bf16)
    edge = pltpu.VMEM((count_s, halo, cells), bf16)
    values = far_away(forcing.reshape(count_s, rows, cells))
    forcings = [None] * count_s
    forcings[early[0]], forcings[early[1]] = pl.pallas_call(
        functools.partial(split_kernel, picks=early),
        out_shape=[plane] * 2,
        in_specs=[whole],
        out_specs=[vmem] * 2,
        scratch_shapes=[pltpu.SemaphoreType.DMA((2,))],
        compiler_params=pltpu.CompilerParams(vmem_limit_bytes=GRANT),
        name="split",
    )(values)
    *others, last, first = pl.pallas_call(
        functools.partial(edges_kernel, picks=late),
        out_shape=[plane] * len(late) + [edge] * 2,
        in_specs=[whole],
        out_specs=[vmem] * (len(late) + 2),
        scratch_shapes=[pltpu.SemaphoreType.DMA((len(late) + 2,))],
        compiler_params=pltpu.CompilerParams(vmem_limit_bytes=GRANT),
        name="edges",
    )(values)
    for s, other in zip(late, others):
        forcings[s] = other

    mean = mean_flow.reshape(1, cells)
    flows = []
    for s in range(count_s // 2):
        beside = lax.ppermute(forcings[s], "space", swap)
        beyond = lax.ppermute(beside, "space", [(j, i) for i, j in apart])
        flows += [beside, beyond]
    for s in range(count_s // 2, count_s):
        beyond = lax.ppermute(forcings[s], "space", apart)
        both = pl.pallas_call(
            functools.partial(join_kernel, slabs=slabs),
            out_shape=pltpu.VMEM((rows, cells), bf16),
            in_specs=[vmem, vmem, vmem, smem],
            out_specs=vmem,
            compiler_params=pltpu.CompilerParams(vmem_limit_bytes=GRANT),
            name="join",
        )(*near(forcings[s], beyond, mean), slab)
        flows.append(lax.ppermute(both, "space", swap))

    one = lax.ppermute(last, "freq", [(i, (i + 1) % blocks) for i in range(blocks)])
    other = lax.ppermute(first, "freq", [((i + 1) % blocks, i) for i in range(blocks)])
    before, after = one, other

    mixed_rows = (MODES + 1) * rows
    width = 2 * (rows + 2 * HALO_ROWS)
    *starts, weights = pl.pallas_call(
        functools.partial(prepare_kernel, count_s=count_s, count_h=count_h, blocks=blocks),
        out_shape=[pltpu.VMEM((rows, cells), f32)] * count_s + [pltpu.VMEM((mixed_rows, width), bf16)],
        in_specs=[vmem] * count_s + [smem] * 4,
        out_specs=[vmem] * (count_s + 1),
        scratch_shapes=[pltpu.VMEM((NZ // math.gcd(LANES, NZ), 3 * LANES, LANES), bf16)],
        compiler_params=pltpu.CompilerParams(vmem_limit_bytes=GRANT),
        name="prepare",
    )(*near(*forcings), mixing.transpose(1, 2, 0), couple_flags, harm_lo, block)

    parts = []
    for s in range(count_s):
        part = pl.pallas_call(
            functools.partial(couple_kernel, at_s=s, count_h=count_h),
            out_shape=pltpu.VMEM((rows, cells), f32),
            in_specs=[vmem] * 6,
            out_specs=vmem,
            scratch_shapes=[pltpu.VMEM((width, cells), bf16)],
            compiler_params=pltpu.CompilerParams(vmem_limit_bytes=GRANT),
            name="couple",
        )(*near(forcings[s], before, after, weights, base_harm, starts[s]))
        parts.append(part)

    cells_all = count_h * blocks * 2 * V * planes * slabs * cells
    response, gram = pl.pallas_call(
        functools.partial(finish_kernel, count_s=count_s, slabs=slabs, scale=1.0 / cells_all),
        out_shape=[pltpu.VMEM((count_s, rows, cells), bf16), pltpu.VMEM((count_s, count_s), f32)],
        in_specs=[vmem, smem] + [vmem] * (count_s + len(flows)),
        out_specs=[vmem] * 2,
        compiler_params=pltpu.CompilerParams(vmem_limit_bytes=GRANT),
        name="finish",
    )(*near(mean), slab, *near(*parts, *flows))
    copies = jnp.broadcast_to(gram, (slabs * blocks, count_s, count_s))
    grams = lax.all_to_all(copies, ("space", "freq"), 0, 0)
    return response.reshape(forcing.shape), jnp.sum(grams, axis=0)


def solution(mesh):
    return jax.shard_map(
        local,
        mesh=mesh,
        in_specs=(
            P(None, "freq", None, "space", None),
            P(None, None, "space", None),
            P(),
            P(),
            P(),
            P("freq", None),
        ),
        out_specs=(P(None, "freq", None, "space", None), P()),
        check_vma=False,
    )
```

```python
import functools
import math

import jax
import jax.numpy as jnp
from jax import lax
from jax.experimental import pallas as pl
from jax.experimental.pallas import tpu as pltpu
from jax.sharding import PartitionSpec as P


V = 4
NZ = 48
MODES = 7
REACH = 3

OMEGA = 0.05
VISCOSITY = 0.25

TILE = 256
LANES = 128
GRANT = 8 * 2**20
HALO_ROWS = 32


def split_kernel(f_ref, *refs, picks):
    *outs, sems = refs
    copies = [pltpu.make_async_copy(f_ref.at[s], out, sems.at[i]) for i, (s, out) in enumerate(zip(picks, outs))]
    for copy in copies:
        copy.start()
    for copy in copies:
        copy.wait()


def edges_kernel(f_ref, *refs, picks):
    *outs, last_ref, first_ref, sems = refs
    rows, halo = f_ref.shape[1], last_ref.shape[1]
    copies = [
        pltpu.make_async_copy(f_ref.at[:, rows - halo : rows], last_ref, sems.at[0]),
        pltpu.make_async_copy(f_ref.at[:, 0:halo], first_ref, sems.at[1]),
    ]
    for i, (s, out) in enumerate(zip(picks, outs)):
        copies.append(pltpu.make_async_copy(f_ref.at[s], out, sems.at[2 + i]))
    for copy in copies:
        copy.start()
    for copy in copies:
        copy.wait()


def gains(mean_ref, slab_ref, slabs):
    slab = slab_ref[0]
    odd = slab % 2 == 1
    inside = jnp.where(odd, slab < slabs - 1, slab > 0).astype(jnp.float32)
    tilt = jnp.where(odd, 0.5, -0.5).astype(jnp.float32) * mean_ref[...]
    return VISCOSITY + tilt, (VISCOSITY - tilt) * inside


def join_kernel(own_ref, far_ref, mean_ref, slab_ref, out_ref, *, slabs):
    slab = slab_ref[0]
    odd = slab % 2 == 1
    inside = jnp.where(odd, slab > 1, slab < slabs - 2).astype(jnp.float32)
    tilt = jnp.where(odd, -0.5, 0.5).astype(jnp.float32) * mean_ref[...]
    far_gain = (VISCOSITY - tilt) * inside
    total = (VISCOSITY + tilt) * own_ref[...].astype(jnp.float32)
    total = total + far_gain * far_ref[...].astype(jnp.float32)
    out_ref[...] = total.astype(jnp.bfloat16)


def prepare_kernel(*refs, count_s, count_h, blocks):
    f32 = jnp.float32
    f_refs = refs[:count_s]
    mix_ref, flag_ref, low_ref, block_ref = refs[count_s : count_s + 4]
    *acc_refs, w_ref, lap_ref = refs[count_s + 4 :]
    rows, cells = f_refs[0].shape
    phases = lap_ref.shape[0]
    for p in range(phases):
        start = (p * LANES) % NZ
        source = lax.broadcasted_iota(jnp.int32, (3 * LANES, LANES), 0) + (start - LANES)
        target = lax.broadcasted_iota(jnp.int32, (1, LANES), 1) + start
        pos = target % NZ
        up = jnp.where(pos == NZ - 1, target - (NZ - 1), target + 1)
        down = jnp.where(pos == 0, target + (NZ - 1), target - 1)
        gap = jnp.abs(source - target)
        near = (source == up) | (source == down) | (gap == NZ)
        block = jnp.where(gap == 0, 6.0 * VISCOSITY, jnp.where(near, -VISCOSITY, 0.0))
        lap_ref[p] = block.astype(jnp.bfloat16)
    steps = cells // LANES
    for j in range(steps):
        low, high = max(j - 1, 0), min(j + 2, steps)
        weights = lap_ref[j % phases, (low - j + 1) * LANES : (high - j + 1) * LANES, :]
        for f_ref, acc_ref in zip(f_refs, acc_refs):
            acc_ref[:, j * LANES : (j + 1) * LANES] = jnp.dot(
                f_ref[:, low * LANES : high * LANES], weights, preferred_element_type=f32
            )

    width = rows + 2 * HALO_ROWS
    row = lax.broadcasted_iota(jnp.int32, (8, width), 0)
    col = lax.broadcasted_iota(jnp.int32, (8, width), 1)
    row_v, col_v = row % V, col % V
    same = (row // V) == ((col // V) % 2)
    harm = col // 8

    def put(at, value):
        high = value.astype(jnp.bfloat16)
        low = (value - high.astype(f32)).astype(jnp.bfloat16)
        w_ref[at : at + 16, 0:width] = high
        w_ref[at : at + 16, width : 2 * width] = low

    def slab(k):
        if k < 0:
            return count_h + (k + REACH)
        if k >= count_h:
            return count_h + HALO_ROWS // 8 + (k - count_h)
        return k

    def two(tile):
        return jnp.concatenate([tile(0), tile(1)], axis=0)

    reached = jnp.where(
        harm < count_h,
        1.0,
        jnp.where(
            harm < count_h + HALO_ROWS // 8,
            (block_ref[0] > 0).astype(f32),
            (block_ref[0] < blocks - 1).astype(f32),
        ),
    )
    for m in range(MODES):
        mixed = jnp.zeros((8, width), f32)
        for v in range(V):
            for w in range(V):
                mixed = jnp.where((row_v == v) & (col_v == w), -mix_ref[v, w, m], mixed)
        mixed = jnp.where(same, mixed, 0.0) * reached
        for k in range(0, count_h, 2):
            put(
                (m * count_h + k) * 8,
                two(
                    lambda i: jnp.where(
                        harm == slab(k + i - (m - REACH)),
                        mixed * flag_ref[k + i, m].astype(f32),
                        0.0,
                    )
                ),
            )
    sign = jnp.where(row < V, -1.0, 1.0)
    first = low_ref[0] + block_ref[0] * count_h
    crossed = (row_v == col_v) & jnp.logical_not(same)
    for k in range(0, count_h, 2):
        put(
            (MODES * count_h + k) * 8,
            two(
                lambda i: jnp.where(
                    crossed & (harm == k + i), sign * (OMEGA * (first + k + i).astype(f32)), 0.0
                )
            ),
        )


def couple_kernel(f_ref, before_ref, after_ref, w_ref, base_ref, start_ref, out_ref, x_ref, *, at_s, count_h):
    f32 = jnp.float32
    rows, cells = f_ref.shape
    width = rows + 2 * HALO_ROWS
    empty = jnp.zeros((HALO_ROWS - REACH * 8, cells), f32)
    around = jnp.concatenate(
        [before_ref[at_s].astype(f32), empty, after_ref[at_s].astype(f32), empty], axis=0
    ).astype(jnp.bfloat16)
    own = f_ref[...]
    for at in (0, width):
        x_ref[at : at + rows, :] = own
        x_ref[at + rows : at + width, :] = around
    row = lax.broadcasted_iota(jnp.int32, (8, TILE), 0)
    for j in range(cells // TILE):
        cut = slice(j * TILE, (j + 1) * TILE)
        mixed = jnp.dot(w_ref[...], x_ref[:, cut], preferred_element_type=f32)
        real = [jnp.broadcast_to(base_ref[m, 0, :, cut], (8, TILE)) for m in range(MODES)]
        imag = [jnp.broadcast_to(base_ref[m, 1, :, cut], (8, TILE)) for m in range(MODES)]
        imag = [jnp.where(row < V, b, -b) for b in imag]
        for k in range(count_h):
            at = (MODES * count_h + k) * 8
            straight = start_ref[k * 8 : k * 8 + 8, cut] + mixed[at : at + 8]
            crossed = None
            for m in range(MODES):
                at = (m * count_h + k) * 8
                straight = straight + real[m] * mixed[at : at + 8]
                turn = imag[m] * mixed[at : at + 8]
                crossed = turn if crossed is None else crossed + turn
            out_ref[k * 8 : k * 8 + 8, cut] = straight + pltpu.roll(crossed, V, 0)


def finish_kernel(*refs, count_s, slabs, scale):
    f32 = jnp.float32
    mean_ref, slab_ref, *refs = refs
    parts, flows = refs[:count_s], refs[count_s:-2]
    out_ref, gram_ref = refs[-2:]
    rows, cells = parts[0].shape
    pairs = [(s, t) for s in range(count_s) for t in range(s, count_s)]
    sums = [None] * len(pairs)
    near_gain, far_gain = gains(mean_ref, slab_ref, slabs)
    for c in range(0, cells, LANES):
        cut = slice(c, c + LANES)
        near_here = jnp.broadcast_to(near_gain[:, cut], (16, LANES))
        far_here = jnp.broadcast_to(far_gain[:, cut], (16, LANES))
        for r in range(0, rows, 16):
            values = []
            for s in range(count_s):
                value = parts[s][r : r + 16, cut]
                if s < count_s // 2:
                    value = value - near_here * flows[2 * s][r : r + 16, cut].astype(f32)
                    value = value - far_here * flows[2 * s + 1][r : r + 16, cut].astype(f32)
                else:
                    value = value - flows[s + count_s // 2][r : r + 16, cut].astype(f32)
                value = value.astype(jnp.bfloat16)
                out_ref[s, r : r + 16, cut] = value
                values.append(value.astype(f32))
            for p, (s, t) in enumerate(pairs):
                product = values[s] * values[t]
                sums[p] = product if sums[p] is None else sums[p] + product
    at_s = lax.broadcasted_iota(jnp.int32, (count_s, count_s), 0)
    at_t = lax.broadcasted_iota(jnp.int32, (count_s, count_s), 1)
    gram = jnp.zeros((count_s, count_s), f32)
    for (s, t), total in zip(pairs, sums):
        value = jnp.sum(total, keepdims=True) * scale
        here = ((at_s == s) & (at_t == t)) | ((at_s == t) & (at_t == s))
        gram = jnp.where(here, value, gram)
    gram_ref[...] = gram


def near(*values):
    return [pltpu.with_memory_space_constraint(value, pltpu.VMEM) for value in values]


def far_away(value):
    return pltpu.with_memory_space_constraint(value, pltpu.HBM)


def local(forcing, base_harm, mixing, mean_flow, harm_lo, couple_flags):
    count_s, count_h, _, planes, cells = forcing.shape
    slabs = lax.axis_size("space")
    blocks = lax.axis_size("freq")
    assert planes == 1 and slabs % 2 == 0 and count_h % 2 == 0
    rows = count_h * 2 * V
    halo = REACH * 2 * V
    f32, bf16 = jnp.float32, jnp.bfloat16
    vmem = pl.BlockSpec(memory_space=pltpu.VMEM)
    smem = pl.BlockSpec(memory_space=pltpu.SMEM)
    whole = pl.BlockSpec(memory_space=pl.ANY)
    slab = lax.axis_index("space").reshape(1)
    block = lax.axis_index("freq").reshape(1)

    apart = [(i, (i + 2 if i % 2 else i - 2) % slabs) for i in range(slabs)]
    inside = [(i, j) for i in range(slabs) if 0 <= (j := i + 2 if i % 2 else i - 2) < slabs]
    last_of_half = (count_s // 2 - 1, count_s - 1)
    swap = [(i, i ^ 1) for i in range(slabs)]

    early = [0, count_s // 2]
    late = [s for s in range(count_s) if s not in early]
    plane = pltpu.VMEM((rows, cells), bf16)
    edge = pltpu.VMEM((count_s, halo, cells), bf16)
    values = far_away(forcing.reshape(count_s, rows, cells))
    forcings = [None] * count_s
    forcings[early[0]], forcings[early[1]] = pl.pallas_call(
        functools.partial(split_kernel, picks=early),
        out_shape=[plane] * 2,
        in_specs=[whole],
        out_specs=[vmem] * 2,
        scratch_shapes=[pltpu.SemaphoreType.DMA((2,))],
        compiler_params=pltpu.CompilerParams(vmem_limit_bytes=GRANT),
        name="split",
    )(values)
    *others, last, first = pl.pallas_call(
        functools.partial(edges_kernel, picks=late),
        out_shape=[plane] * len(late) + [edge] * 2,
        in_specs=[whole],
        out_specs=[vmem] * (len(late) + 2),
        scratch_shapes=[pltpu.SemaphoreType.DMA((len(late) + 2,))],
        compiler_params=pltpu.CompilerParams(vmem_limit_bytes=GRANT),
        name="edges",
    )(values)
    for s, other in zip(late, others):
        forcings[s] = other

    mean = mean_flow.reshape(1, cells)
    flows = []
    for s in range(count_s // 2):
        beside = lax.ppermute(forcings[s], "space", swap)
        pairs = inside if s in last_of_half else apart
        beyond = lax.ppermute(beside, "space", [(j, i) for i, j in pairs])
        flows += [beside, beyond]
    for s in range(count_s // 2, count_s):
        pairs = inside if s in last_of_half else apart
        beyond = lax.ppermute(forcings[s], "space", pairs)
        both = pl.pallas_call(
            functools.partial(join_kernel, slabs=slabs),
            out_shape=pltpu.VMEM((rows, cells), bf16),
            in_specs=[vmem, vmem, vmem, smem],
            out_specs=vmem,
            compiler_params=pltpu.CompilerParams(vmem_limit_bytes=GRANT),
            name="join",
        )(*near(forcings[s], beyond, mean), slab)
        flows.append(lax.ppermute(both, "space", swap))

    one = lax.ppermute(last, "freq", [(i, (i + 1) % blocks) for i in range(blocks)])
    other = lax.ppermute(first, "freq", [((i + 1) % blocks, i) for i in range(blocks)])
    before, after = one, other

    mixed_rows = (MODES + 1) * rows
    width = 2 * (rows + 2 * HALO_ROWS)
    *starts, weights = pl.pallas_call(
        functools.partial(prepare_kernel, count_s=count_s, count_h=count_h, blocks=blocks),
        out_shape=[pltpu.VMEM((rows, cells), f32)] * count_s + [pltpu.VMEM((mixed_rows, width), bf16)],
        in_specs=[vmem] * count_s + [smem] * 4,
        out_specs=[vmem] * (count_s + 1),
        scratch_shapes=[pltpu.VMEM((NZ // math.gcd(LANES, NZ), 3 * LANES, LANES), bf16)],
        compiler_params=pltpu.CompilerParams(vmem_limit_bytes=GRANT),
        name="prepare",
    )(*near(*forcings), mixing.transpose(1, 2, 0), couple_flags, harm_lo, block)

    parts = []
    for s in range(count_s):
        part = pl.pallas_call(
            functools.partial(couple_kernel, at_s=s, count_h=count_h),
            out_shape=pltpu.VMEM((rows, cells), f32),
            in_specs=[vmem] * 6,
            out_specs=vmem,
            scratch_shapes=[pltpu.VMEM((width, cells), bf16)],
            compiler_params=pltpu.CompilerParams(vmem_limit_bytes=GRANT),
            name="couple",
        )(*near(forcings[s], before, after, weights, base_harm, starts[s]))
        parts.append(part)

    cells_all = count_h * blocks * 2 * V * planes * slabs * cells
    response, gram = pl.pallas_call(
        functools.partial(finish_kernel, count_s=count_s, slabs=slabs, scale=1.0 / cells_all),
        out_shape=[jax.ShapeDtypeStruct((count_s, rows, cells), bf16), pltpu.VMEM((count_s, count_s), f32)],
        in_specs=[vmem, smem] + [vmem] * (count_s + len(flows)),
        out_specs=[vmem] * 2,
        compiler_params=pltpu.CompilerParams(vmem_limit_bytes=GRANT),
        name="finish",
    )(*near(mean), slab, *near(*parts, *flows))
    copies = jnp.broadcast_to(gram, (slabs * blocks, count_s, count_s))
    grams = lax.all_to_all(copies, ("space", "freq"), 0, 0)
    return response.reshape(forcing.shape), jnp.sum(grams, axis=0)


def solution(mesh):
    return jax.shard_map(
        local,
        mesh=mesh,
        in_specs=(
            P(None, "freq", None, "space", None),
            P(None, None, "space", None),
            P(),
            P(),
            P(),
            P("freq", None),
        ),
        out_specs=(P(None, "freq", None, "space", None), P()),
        check_vma=False,
    )
```

```python
import functools
import math

import jax
import jax.numpy as jnp
from jax import lax
from jax.experimental import pallas as pl
from jax.experimental.pallas import tpu as pltpu
from jax.sharding import PartitionSpec as P


V = 4
NZ = 48
MODES = 7
REACH = 3

OMEGA = 0.05
VISCOSITY = 0.25

TILE = 256
LANES = 128
GRANT = 8 * 2**20
HALO_ROWS = 32


def split_kernel(f_ref, *refs, picks):
    *outs, sems = refs
    copies = [pltpu.make_async_copy(f_ref.at[s], out, sems.at[i]) for i, (s, out) in enumerate(zip(picks, outs))]
    for copy in copies:
        copy.start()
    for copy in copies:
        copy.wait()


def edges_kernel(f_ref, *refs, picks):
    *outs, last_ref, first_ref, sems = refs
    rows, halo = f_ref.shape[1], last_ref.shape[1]
    copies = [
        pltpu.make_async_copy(f_ref.at[:, rows - halo : rows], last_ref, sems.at[0]),
        pltpu.make_async_copy(f_ref.at[:, 0:halo], first_ref, sems.at[1]),
    ]
    for i, (s, out) in enumerate(zip(picks, outs)):
        copies.append(pltpu.make_async_copy(f_ref.at[s], out, sems.at[2 + i]))
    for copy in copies:
        copy.start()
    for copy in copies:
        copy.wait()


def gains(mean_ref, slab_ref, slabs):
    slab = slab_ref[0]
    odd = slab % 2 == 1
    inside = jnp.where(odd, slab < slabs - 1, slab > 0).astype(jnp.float32)
    tilt = jnp.where(odd, 0.5, -0.5).astype(jnp.float32) * mean_ref[...]
    return VISCOSITY + tilt, (VISCOSITY - tilt) * inside


def join_kernel(own_ref, far_ref, mean_ref, slab_ref, out_ref, *, slabs):
    slab = slab_ref[0]
    odd = slab % 2 == 1
    inside = jnp.where(odd, slab > 1, slab < slabs - 2).astype(jnp.float32)
    tilt = jnp.where(odd, -0.5, 0.5).astype(jnp.float32) * mean_ref[...]
    far_gain = (VISCOSITY - tilt) * inside
    total = (VISCOSITY + tilt) * own_ref[...].astype(jnp.float32)
    total = total + far_gain * far_ref[...].astype(jnp.float32)
    out_ref[...] = total.astype(jnp.bfloat16)


def prepare_kernel(*refs, count_s, count_h, blocks):
    f32 = jnp.float32
    f_refs = refs[:count_s]
    mix_ref, flag_ref, low_ref, block_ref = refs[count_s : count_s + 4]
    *acc_refs, w_ref, lap_ref = refs[count_s + 4 :]
    rows, cells = f_refs[0].shape
    phases = lap_ref.shape[0]
    for p in range(phases):
        start = (p * LANES) % NZ
        source = lax.broadcasted_iota(jnp.int32, (3 * LANES, LANES), 0) + (start - LANES)
        target = lax.broadcasted_iota(jnp.int32, (1, LANES), 1) + start
        pos = target % NZ
        up = jnp.where(pos == NZ - 1, target - (NZ - 1), target + 1)
        down = jnp.where(pos == 0, target + (NZ - 1), target - 1)
        gap = jnp.abs(source - target)
        near = (source == up) | (source == down) | (gap == NZ)
        block = jnp.where(gap == 0, 6.0 * VISCOSITY, jnp.where(near, -VISCOSITY, 0.0))
        lap_ref[p] = block.astype(jnp.bfloat16)
    steps = cells // LANES
    for j in range(steps):
        low, high = max(j - 1, 0), min(j + 2, steps)
        weights = lap_ref[j % phases, (low - j + 1) * LANES : (high - j + 1) * LANES, :]
        for f_ref, acc_ref in zip(f_refs, acc_refs):
            acc_ref[:, j * LANES : (j + 1) * LANES] = jnp.dot(
                f_ref[:, low * LANES : high * LANES], weights, preferred_element_type=f32
            )

    width = rows + 2 * HALO_ROWS
    row = lax.broadcasted_iota(jnp.int32, (8, width), 0)
    col = lax.broadcasted_iota(jnp.int32, (8, width), 1)
    row_v, col_v = row % V, col % V
    same = (row // V) == ((col // V) % 2)
    harm = col // 8

    def put(at, value):
        high = value.astype(jnp.bfloat16)
        low = (value - high.astype(f32)).astype(jnp.bfloat16)
        w_ref[at : at + 16, 0:width] = high
        w_ref[at : at + 16, width : 2 * width] = low

    def slab(k):
        if k < 0:
            return count_h + (k + REACH)
        if k >= count_h:
            return count_h + HALO_ROWS // 8 + (k - count_h)
        return k

    def two(tile):
        return jnp.concatenate([tile(0), tile(1)], axis=0)

    reached = jnp.where(
        harm < count_h,
        1.0,
        jnp.where(
            harm < count_h + HALO_ROWS // 8,
            (block_ref[0] > 0).astype(f32),
            (block_ref[0] < blocks - 1).astype(f32),
        ),
    )
    for m in range(MODES):
        mixed = jnp.zeros((8, width), f32)
        for v in range(V):
            for w in range(V):
                mixed = jnp.where((row_v == v) & (col_v == w), -mix_ref[v, w, m], mixed)
        mixed = jnp.where(same, mixed, 0.0) * reached
        for k in range(0, count_h, 2):
            put(
                (m * count_h + k) * 8,
                two(
                    lambda i: jnp.where(
                        harm == slab(k + i - (m - REACH)),
                        mixed * flag_ref[k + i, m].astype(f32),
                        0.0,
                    )
                ),
            )
    sign = jnp.where(row < V, -1.0, 1.0)
    first = low_ref[0] + block_ref[0] * count_h
    crossed = (row_v == col_v) & jnp.logical_not(same)
    for k in range(0, count_h, 2):
        put(
            (MODES * count_h + k) * 8,
            two(
                lambda i: jnp.where(
                    crossed & (harm == k + i), sign * (OMEGA * (first + k + i).astype(f32)), 0.0
                )
            ),
        )


def couple_kernel(f_ref, before_ref, after_ref, w_ref, base_ref, start_ref, out_ref, x_ref, *, at_s, count_h):
    f32 = jnp.float32
    rows, cells = f_ref.shape
    width = rows + 2 * HALO_ROWS
    empty = jnp.zeros((HALO_ROWS - REACH * 8, cells), f32)
    around = jnp.concatenate(
        [before_ref[at_s].astype(f32), empty, after_ref[at_s].astype(f32), empty], axis=0
    ).astype(jnp.bfloat16)
    own = f_ref[...]
    for at in (0, width):
        x_ref[at : at + rows, :] = own
        x_ref[at + rows : at + width, :] = around
    row = lax.broadcasted_iota(jnp.int32, (8, TILE), 0)
    for j in range(cells // TILE):
        cut = slice(j * TILE, (j + 1) * TILE)
        mixed = jnp.dot(w_ref[...], x_ref[:, cut], preferred_element_type=f32)
        real = [jnp.broadcast_to(base_ref[m, 0, :, cut], (8, TILE)) for m in range(MODES)]
        imag = [jnp.broadcast_to(base_ref[m, 1, :, cut], (8, TILE)) for m in range(MODES)]
        imag = [jnp.where(row < V, b, -b) for b in imag]
        for k in range(count_h):
            at = (MODES * count_h + k) * 8
            straight = start_ref[k * 8 : k * 8 + 8, cut] + mixed[at : at + 8]
            crossed = None
            for m in range(MODES):
                at = (m * count_h + k) * 8
                straight = straight + real[m] * mixed[at : at + 8]
                turn = imag[m] * mixed[at : at + 8]
                crossed = turn if crossed is None else crossed + turn
            out_ref[k * 8 : k * 8 + 8, cut] = straight + pltpu.roll(crossed, V, 0)


def finish_kernel(*refs, count_s, slabs, scale):
    f32 = jnp.float32
    mean_ref, slab_ref, *refs = refs
    *refs, out_ref, gram_ref, held_ref, sems = refs
    parts, flows = refs[:count_s], refs[count_s:]
    rows, cells = parts[0].shape
    pairs = [(s, t) for s in range(count_s) for t in range(s, count_s)]
    sums = [None] * len(pairs)
    near_gain, far_gain = gains(mean_ref, slab_ref, slabs)
    copies = []
    for r in range(0, rows, 16):
        for c in range(0, cells, LANES):
            cut = slice(c, c + LANES)
            near_here = jnp.broadcast_to(near_gain[:, cut], (16, LANES))
            far_here = jnp.broadcast_to(far_gain[:, cut], (16, LANES))
            values = []
            for s in range(count_s):
                value = parts[s][r : r + 16, cut]
                if s < count_s // 2:
                    value = value - near_here * flows[2 * s][r : r + 16, cut].astype(f32)
                    value = value - far_here * flows[2 * s + 1][r : r + 16, cut].astype(f32)
                else:
                    value = value - flows[s + count_s // 2][r : r + 16, cut].astype(f32)
                value = value.astype(jnp.bfloat16)
                held_ref[s, r : r + 16, cut] = value
                values.append(value.astype(f32))
            for p, (s, t) in enumerate(pairs):
                product = values[s] * values[t]
                sums[p] = product if sums[p] is None else sums[p] + product
        ready = (slice(None), slice(r, r + 16))
        copies.append(pltpu.make_async_copy(held_ref.at[ready], out_ref.at[ready], sems.at[r // 16]))
        copies[-1].start()
    at_s = lax.broadcasted_iota(jnp.int32, (count_s, count_s), 0)
    at_t = lax.broadcasted_iota(jnp.int32, (count_s, count_s), 1)
    gram = jnp.zeros((count_s, count_s), f32)
    for (s, t), total in zip(pairs, sums):
        value = jnp.sum(total, keepdims=True) * scale
        here = ((at_s == s) & (at_t == t)) | ((at_s == t) & (at_t == s))
        gram = jnp.where(here, value, gram)
    gram_ref[...] = gram
    for copy in copies:
        copy.wait()


def near(*values):
    return [pltpu.with_memory_space_constraint(value, pltpu.VMEM) for value in values]


def far_away(value):
    return pltpu.with_memory_space_constraint(value, pltpu.HBM)


def local(forcing, base_harm, mixing, mean_flow, harm_lo, couple_flags):
    count_s, count_h, _, planes, cells = forcing.shape
    slabs = lax.axis_size("space")
    blocks = lax.axis_size("freq")
    assert planes == 1 and slabs % 2 == 0 and count_h % 2 == 0
    rows = count_h * 2 * V
    halo = REACH * 2 * V
    f32, bf16 = jnp.float32, jnp.bfloat16
    vmem = pl.BlockSpec(memory_space=pltpu.VMEM)
    smem = pl.BlockSpec(memory_space=pltpu.SMEM)
    whole = pl.BlockSpec(memory_space=pl.ANY)
    slab = lax.axis_index("space").reshape(1)
    block = lax.axis_index("freq").reshape(1)

    apart = [(i, (i + 2 if i % 2 else i - 2) % slabs) for i in range(slabs)]
    inside = [(i, j) for i in range(slabs) if 0 <= (j := i + 2 if i % 2 else i - 2) < slabs]
    last_of_half = (count_s // 2 - 1, count_s - 1)
    swap = [(i, i ^ 1) for i in range(slabs)]

    early = [0, count_s // 2]
    late = [s for s in range(count_s) if s not in early]
    plane = pltpu.VMEM((rows, cells), bf16)
    edge = pltpu.VMEM((count_s, halo, cells), bf16)
    values = far_away(forcing.reshape(count_s, rows, cells))
    forcings = [None] * count_s
    forcings[early[0]], forcings[early[1]] = pl.pallas_call(
        functools.partial(split_kernel, picks=early),
        out_shape=[plane] * 2,
        in_specs=[whole],
        out_specs=[vmem] * 2,
        scratch_shapes=[pltpu.SemaphoreType.DMA((2,))],
        compiler_params=pltpu.CompilerParams(vmem_limit_bytes=GRANT),
        name="split",
    )(values)
    *others, last, first = pl.pallas_call(
        functools.partial(edges_kernel, picks=late),
        out_shape=[plane] * len(late) + [edge] * 2,
        in_specs=[whole],
        out_specs=[vmem] * (len(late) + 2),
        scratch_shapes=[pltpu.SemaphoreType.DMA((len(late) + 2,))],
        compiler_params=pltpu.CompilerParams(vmem_limit_bytes=GRANT),
        name="edges",
    )(values)
    for s, other in zip(late, others):
        forcings[s] = other

    mean = mean_flow.reshape(1, cells)
    flows = []
    for s in range(count_s // 2):
        beside = lax.ppermute(forcings[s], "space", swap)
        pairs = inside if s in last_of_half else apart
        beyond = lax.ppermute(beside, "space", [(j, i) for i, j in pairs])
        flows += [beside, beyond]
    for s in range(count_s // 2, count_s):
        pairs = inside if s in last_of_half else apart
        beyond = lax.ppermute(forcings[s], "space", pairs)
        both = pl.pallas_call(
            functools.partial(join_kernel, slabs=slabs),
            out_shape=pltpu.VMEM((rows, cells), bf16),
            in_specs=[vmem, vmem, vmem, smem],
            out_specs=vmem,
            compiler_params=pltpu.CompilerParams(vmem_limit_bytes=GRANT),
            name="join",
        )(*near(forcings[s], beyond, mean), slab)
        flows.append(lax.ppermute(both, "space", swap))

    one = lax.ppermute(last, "freq", [(i, (i + 1) % blocks) for i in range(blocks)])
    other = lax.ppermute(first, "freq", [((i + 1) % blocks, i) for i in range(blocks)])
    before, after = one, other

    mixed_rows = (MODES + 1) * rows
    width = 2 * (rows + 2 * HALO_ROWS)
    *starts, weights = pl.pallas_call(
        functools.partial(prepare_kernel, count_s=count_s, count_h=count_h, blocks=blocks),
        out_shape=[pltpu.VMEM((rows, cells), f32)] * count_s + [pltpu.VMEM((mixed_rows, width), bf16)],
        in_specs=[vmem] * count_s + [smem] * 4,
        out_specs=[vmem] * (count_s + 1),
        scratch_shapes=[pltpu.VMEM((NZ // math.gcd(LANES, NZ), 3 * LANES, LANES), bf16)],
        compiler_params=pltpu.CompilerParams(vmem_limit_bytes=GRANT),
        name="prepare",
    )(*near(*forcings), mixing.transpose(1, 2, 0), couple_flags, harm_lo, block)

    parts = []
    for s in range(count_s):
        part = pl.pallas_call(
            functools.partial(couple_kernel, at_s=s, count_h=count_h),
            out_shape=pltpu.VMEM((rows, cells), f32),
            in_specs=[vmem] * 6,
            out_specs=vmem,
            scratch_shapes=[pltpu.VMEM((width, cells), bf16)],
            compiler_params=pltpu.CompilerParams(vmem_limit_bytes=GRANT),
            name="couple",
        )(*near(forcings[s], before, after, weights, base_harm, starts[s]))
        parts.append(part)

    cells_all = count_h * blocks * 2 * V * planes * slabs * cells
    response, gram = pl.pallas_call(
        functools.partial(finish_kernel, count_s=count_s, slabs=slabs, scale=1.0 / cells_all),
        out_shape=[pltpu.HBM((count_s, rows, cells), bf16), pltpu.VMEM((count_s, count_s), f32)],
        in_specs=[vmem, smem] + [vmem] * (count_s + len(flows)),
        out_specs=[whole, vmem],
        scratch_shapes=[
            pltpu.VMEM((count_s, rows, cells), bf16),
            pltpu.SemaphoreType.DMA((rows // 16,)),
        ],
        compiler_params=pltpu.CompilerParams(vmem_limit_bytes=GRANT),
        name="finish",
    )(*near(mean), slab, *near(*parts, *flows))
    copies = jnp.broadcast_to(gram, (slabs * blocks, count_s, count_s))
    grams = lax.all_to_all(copies, ("space", "freq"), 0, 0)
    return response.reshape(forcing.shape), jnp.sum(grams, axis=0)


def solution(mesh):
    return jax.shard_map(
        local,
        mesh=mesh,
        in_specs=(
            P(None, "freq", None, "space", None),
            P(None, None, "space", None),
            P(),
            P(),
            P(),
            P("freq", None),
        ),
        out_specs=(P(None, "freq", None, "space", None), P()),
        check_vma=False,
    )
```
